32 devices in a mesh: groups: 2 (over y), cand: 16 (over z, x, core).
Axes of the slice: x: 2, y: 2, z: 4, core: 2. Of those that a mesh axis runs over, the one named last changes fastest.
Arguments:
- correlations: float32 [32768, 2048], P(('groups', 'cand')), parts along dimension 0, may hold values from -1 to 1
- first_inverse: float32 [2048, 1024], P(('groups', 'cand')), parts along dimension 0
- off_block: float32 [2048, 1024], P(('groups', 'cand')), parts along dimension 0, may hold values from -4 to 4
- second_inverse: float32 [2048, 1024], P('groups', 'cand'), parts along dimension 0
- ard_mean: float32 [4096], P('groups'), parts along dimension 0, may hold values from -0.125 to 0.125
- group_ids: int32 [32768, 1], P(('groups', 'cand')), parts along dimension 0, may hold values from 0 to 127
- owner_slots: int32 [256], P('groups'), parts along dimension 0, may hold values from 0 to 127, each once
Outputs:
- energies: float32 [32768], P(('groups', 'cand')), parts along dimension 0
- variances: float32 [32768], P(('groups', 'cand')), parts along dimension 0
- group_energy: float32 [256], P(('groups', 'cand')), parts along dimension 0
- group_variance: float32 [256], P(('groups', 'cand')), parts along dimension 0
The draws below stay inside these ranges and needn't reach their ends.
There are 2 independent parts, one for each index of `groups`. The reference program is written for one: setup_inputs(seed, part) draws one part's arguments, and reference() takes and returns one part's arrays. A program takes and returns all parts, laid end to end along the dimension named above; each array names one. Nothing has to cross between parts.
Inputs may be any that keep to these rules, and one draw needn't show every extreme that they name: `group_ids`: every group has at least one candidate. `owner_slots`: each slot holds exactly one group.
All inputs are finite; a program needn't handle non-finite values.
Results may differ from the reference program's by a relative error of at most 0.0002.
Values sent between devices are 32-bit elements; how exact they have to be, the bound alone decides.
No kernel may reach another device: no remote copies, remote signals or barrier semaphores. Data moves between devices by JAX's collectives and lax.ppermute only.
A program may use at most 128 MiB of HBM per device.

```python
import math
import jax
import jax.numpy as jnp
from jax import lax

E = 2048
PAN = 1024
CANDS = 16384
GROUPS = 128


def lower_factor(key):
    key_off, key_diag, key_rows = jax.random.split(key, 3)
    off_part = jax.random.normal(key_off, (PAN, PAN), jnp.float32)
    diag_part = jax.random.uniform(key_diag, (PAN,), jnp.float32, 0.5, 1.5)
    row_scale = jnp.exp(jax.random.uniform(key_rows, (PAN,), jnp.float32, 0.0, math.log(10.0)))
    strict = jnp.tril(off_part, -1) * (0.7 / math.sqrt(PAN))
    matrix = strict + jnp.diag(diag_part)
    base_scale = 1.0 / math.sqrt(5.0 * E)
    return (matrix * row_scale[:, None] * base_scale).astype(jnp.float32)


def draw_first_inverse(key, part):
    return lower_factor(jax.random.fold_in(key, 11))


def draw_second_inverse(key, part):
    return lower_factor(jax.random.fold_in(key, 23))


def block_scale(stream_key, shape, cuts, smallest, top_value):
    def one(position, shards_of):
        draws = jax.random.uniform(jax.random.fold_in(jax.random.fold_in(stream_key, 6), position), (shards_of,), jnp.float32, smallest / len(cuts), top_value / len(cuts))
        return jnp.repeat(jnp.exp(draws), shape[position] // shards_of).reshape((-1,) + (1,) * (len(shape) - position - 1))

    level = one(*cuts[0])
    for cut in cuts[1:]:
        level = level * one(*cut)
    return level


def distinct(rng, rows, count, top, lift):
    order = jax.random.permutation(jax.random.fold_in(rng, 1), count)
    pull = order
    for power in range(3):
        pull = pull * pull // count
    pull = pull * lift // count
    chance = jax.random.randint(jax.random.fold_in(rng, 2), (rows, count), 0, 4096) + pull
    sure = jax.random.permutation(jax.random.fold_in(rng, 3), rows)[jnp.arange(count) % rows]
    chance = jnp.where(jnp.arange(rows)[:, None] == sure[None, :], 1 << 14, chance)
    priority = chance * count + jnp.arange(count)
    return lax.top_k(priority.astype(jnp.int32), top)[1].astype(jnp.int32)


def gaussian(own_key, shape, width, limit, cuts=(), held_as=jnp.bfloat16):
    values = jax.random.normal(own_key, shape, jnp.float32) * width
    if len(cuts) > 0:
        values = block_scale(own_key, shape, cuts, -0.22, 0.18) * values
    return jnp.clip(values, min=-limit, max=limit).astype(held_as)


def setup_inputs(seed: int = 0, part: int = 0) -> dict:
    keys = jax.random.split(jax.random.key(seed), 8)
    part_keys = jax.random.split(jax.random.fold_in(keys[7], part), 8)
    correlations = jnp.clip(jax.random.uniform(part_keys[0], (CANDS, E), jnp.float32, -1.0, 1.0) * block_scale(part_keys[0], (CANDS, E), ((0, 16),), -0.4, 0.0), -1.0, 1.0)
    first_inverse = draw_first_inverse(jax.random.fold_in(jax.random.fold_in(keys[7], part), 71), part)
    off_block = gaussian(part_keys[2], (PAN, PAN), 0.3, 4.0, ((0, 16),), jnp.float32)
    second_inverse = draw_second_inverse(jax.random.fold_in(jax.random.fold_in(keys[7], part), 71), part)
    ard_mean = gaussian(part_keys[4], (E,), E ** -0.5, 0.125, (), jnp.float32)
    group_ids = distinct(part_keys[5], CANDS, GROUPS, 1, 64)
    owner_slots = jax.random.permutation(part_keys[6], GROUPS).astype(jnp.int32)
    return dict(correlations=correlations, first_inverse=first_inverse, off_block=off_block, second_inverse=second_inverse, ard_mean=ard_mean, group_ids=group_ids, owner_slots=owner_slots)


def matmul_t(left, right):
    return lax.dot_general(left, right, (((1,), (1,)), ((), ())), precision=lax.Precision.HIGHEST, preferred_element_type=jnp.float32)


def reference(correlations, first_inverse, off_block, second_inverse, ard_mean, group_ids, owner_slots):
    leading = correlations[:, :PAN]
    trailing = correlations[:, PAN:]
    first_solve = matmul_t(leading, first_inverse)
    residual = trailing - matmul_t(first_solve, off_block)
    second_solve = matmul_t(residual, second_inverse)
    variances = jnp.sum(first_solve * first_solve, axis=1) + jnp.sum(second_solve * second_solve, axis=1)
    energies = jnp.dot(correlations, ard_mean, precision=lax.Precision.HIGHEST, preferred_element_type=jnp.float32)
    slot_of = owner_slots[group_ids[:, 0]].astype(jnp.int32)
    moments = jnp.stack([energies, variances, jnp.ones_like(energies)], axis=1)
    totals = jax.ops.segment_sum(moments, slot_of, num_segments=GROUPS)
    group_energy = totals[:, 0] / totals[:, 2]
    group_variance = totals[:, 1] / totals[:, 2]
    return energies, variances, group_energy, group_variance
```

```python
import functools

import jax
import jax.numpy as jnp
from jax import lax
from jax.experimental import pallas as pl
from jax.experimental.pallas import tpu as pltpu
from jax.sharding import PartitionSpec as P

LANES = 128
HALVES = 256
BF16, F32 = jnp.bfloat16, jnp.float32


def split(value):
    high = value.astype(BF16)
    return high, (value - high.astype(F32)).astype(BF16)


def product(left, right, contract):
    dims = (((1,), (contract,)), ((), ()))
    one = functools.partial(lax.dot_general, dimension_numbers=dims, preferred_element_type=F32)
    return one(left[0], right[0]) + (one(left[0], right[1]) + one(left[1], right[0]))


def fold(value):
    total = value[:, :LANES]
    for start in range(LANES, value.shape[1], LANES):
        total = total + value[:, start : start + LANES]
    return total


def prepare_kernel(corr_ref, mean_ref, high_ref, low_ref, energy_ref):
    corr = corr_ref[...]
    high_ref[...], low_ref[...] = split(corr[:, : high_ref.shape[1]])
    energy_ref[...] = jnp.sum(fold(corr * mean_ref[...]).T, axis=0, keepdims=True)


def prepare(corr, mean, panel, tile):
    rows, width = corr.shape
    return pl.pallas_call(
        prepare_kernel,
        grid=(rows // tile,),
        in_specs=[
            pl.BlockSpec((tile, width), lambda t: (t, 0)),
            pl.BlockSpec((1, width), lambda t: (0, 0)),
        ],
        out_specs=[
            pl.BlockSpec((tile, panel), lambda t: (t, 0)),
            pl.BlockSpec((tile, panel), lambda t: (t, 0)),
            pl.BlockSpec((1, tile), lambda t: (0, t)),
        ],
        out_shape=[
            jax.ShapeDtypeStruct((rows, panel), BF16),
            jax.ShapeDtypeStruct((rows, panel), BF16),
            jax.ShapeDtypeStruct((1, rows), F32),
        ],
        cost_estimate=pl.CostEstimate(
            flops=2 * rows * width, bytes_accessed=8 * rows * width, transcendentals=0
        ),
        name="prepare",
    )(corr, mean)


def first_kernel(
    ids_ref, m0, o0, m1, o1, high_ref, low_ref,
    fs_high, fs_low, square_ref, solve_high, solve_low, panel_high, panel_low,
):
    panel = high_ref.shape[1]
    core = ids_ref[2]

    @pl.when(pl.program_id(0) == 0)
    def _():
        shard = m0.shape[0]
        for half, pieces in enumerate(((m0, o0), (m1, o1))):
            block = ids_ref[half]
            for piece, row in ((pieces[0], core), (pieces[1], 1 - core)):
                at = pl.ds(pl.multiple_of(half * LANES + row * shard, shard), shard)
                for q in range(panel // LANES):
                    here = slice(q * LANES, (q + 1) * LANES)
                    after = slice((q + 1) * LANES, (q + 2) * LANES)
                    first = jnp.where(q <= block, piece[:, here], 0.0)
                    panel_high[at, here], panel_low[at, here] = split(first)
                    second = jnp.where(q >= block, piece[:, after], 0.0)
                    solve_high[at, here], solve_low[at, here] = split(second)

    last = jnp.maximum(ids_ref[0], ids_ref[1]) // 2
    for k in range(panel // HALVES):

        @pl.when(last == k)
        def _(depth=(k + 1) * HALVES):
            left = high_ref[:, :depth], low_ref[:, :depth]
            right = panel_high[:, :depth], panel_low[:, :depth]
            value = product(left, right, 1)
            fs_high[...], fs_low[...] = split(value)
            square_ref[...] = fold(value * value)


def first_chunk(ids, pieces, high, low, tile):
    rows, panel = high.shape
    whole = lambda t, ids: (0, 0)
    by_tile = lambda t, ids: (t, 0)
    width = 2 * LANES
    return pl.pallas_call(
        first_kernel,
        grid_spec=pltpu.PrefetchScalarGridSpec(
            num_scalar_prefetch=1,
            grid=(rows // tile,),
            in_specs=[pl.BlockSpec(piece.shape, whole) for piece in pieces]
            + [pl.BlockSpec((tile, panel), by_tile)] * 2,
            out_specs=[pl.BlockSpec((tile, width), by_tile)] * 2
            + [pl.BlockSpec((tile, LANES), by_tile)]
            + [pl.BlockSpec((width, panel), whole)] * 2,
            scratch_shapes=[pltpu.VMEM((width, panel), BF16)] * 2,
        ),
        out_shape=[jax.ShapeDtypeStruct((rows, width), BF16)] * 2
        + [jax.ShapeDtypeStruct((rows, LANES), F32)]
        + [jax.ShapeDtypeStruct((width, panel), BF16)] * 2,
        cost_estimate=pl.CostEstimate(
            flops=6 * rows * panel * width, bytes_accessed=4 * rows * panel, transcendentals=0
        ),
        name="first_chunk",
    )(ids, *pieces, high, low)


def second_kernel(chunks, role, ids_ref, *refs):
    m0, o0, m1, o1, trail0, trail1, solve_high, solve_low, *refs = refs
    fs, refs = refs[: 2 * chunks], refs[2 * chunks :]
    if role != "first":
        total_in, *refs = refs
    if role == "last":
        squares, refs = refs[:chunks], refs[chunks:]
        energy_ref, slot_ref, variance_ref, sums_ref, off_high, off_low = refs
    else:
        total_out, off_high, off_low = refs
    panel = solve_high.shape[1]
    core = ids_ref[2]

    @pl.when(pl.program_id(0) == 0)
    def _():
        shard = m0.shape[0]
        for half, pieces in enumerate(((m0, o0), (m1, o1))):
            for piece, row in ((pieces[0], core), (pieces[1], 1 - core)):
                at = pl.ds(pl.multiple_of(half * LANES + row * shard, shard), shard)
                for q in range(2 * chunks):
                    source = pl.ds(pl.multiple_of(ids_ref[3 + q] * LANES, LANES), LANES)
                    here = slice(q * LANES, (q + 1) * LANES)
                    off_high[at, here], off_low[at, here] = split(piece[:, source])

    left = (
        jnp.concatenate([ref[...] for ref in fs[:chunks]], axis=1),
        jnp.concatenate([ref[...] for ref in fs[chunks:]], axis=1),
    )
    residual = jnp.concatenate([trail0[...], trail1[...]], axis=1) - product(
        left, (off_high[...], off_low[...]), 1
    )
    residual = split(residual)
    start = jnp.minimum(ids_ref[0], ids_ref[1]) // 2
    if role != "last":
        for k in range(panel // HALVES):

            @pl.when(start == k)
            def _(begin=k * HALVES):
                value = product(residual, (solve_high[:, begin:], solve_low[:, begin:]), 0)
                if role == "first":
                    if begin:
                        total_out[:, :begin] = jnp.zeros((value.shape[0], begin), F32)
                    total_out[:, begin:] = value
                else:
                    if begin:
                        total_out[:, :begin] = total_in[:, :begin]
                    total_out[:, begin:] = total_in[:, begin:] + value

        return
    value = product(residual, (solve_high[...], solve_low[...]), 0) + total_in[...]
    square = fold(value * value)
    for ref in squares:
        square = square + ref[...]
    variance = jnp.sum(square.T, axis=0, keepdims=True)
    variance_ref[...] = variance

    def three(value):
        high, rest = split(value)
        middle, low = split(value - high.astype(F32))
        del rest
        return [high, middle, low]

    parts = three(energy_ref[...]) + three(variance) + [jnp.ones_like(variance).astype(BF16)]
    moments = jnp.concatenate([part.astype(F32) for part in parts] + [jnp.zeros_like(variance)], axis=0)
    groups = sums_ref.shape[1]
    member = lax.broadcasted_iota(jnp.int32, (groups, variance.shape[1]), 0) == slot_ref[...]
    sums = lax.dot_general(
        moments.astype(BF16),
        member.astype(F32).astype(BF16),
        (((1,), (1,)), ((), ())),
        preferred_element_type=F32,
    )
    sums = jnp.concatenate(
        [sums[0:1] + sums[1:2] + sums[2:3], sums[3:4] + sums[4:5] + sums[5:6], sums[6:7]]
        + [jnp.zeros((5, groups), F32)],
        axis=0,
    )

    @pl.when(pl.program_id(0) == 0)
    def _():
        sums_ref[...] = sums

    @pl.when(pl.program_id(0) != 0)
    def _():
        sums_ref[...] = sums_ref[...] + sums


def second_chunk(role, ids, pieces, corr, solve, fs, tile, total=None, squares=(), rows_in=(), groups=0):
    rows = corr.shape[0]
    panel = solve[0].shape[1]
    chunks = len(fs)
    width = 2 * LANES
    whole = lambda t, ids: (0, 0)
    by_tile = lambda t, ids: (t, 0)
    by_lane = lambda t, ids: (0, t)
    skip = panel // LANES
    operands = [*pieces, corr, corr, *solve, *[pair[0] for pair in fs], *[pair[1] for pair in fs]]
    in_specs = (
        [pl.BlockSpec(piece.shape, whole) for piece in pieces]
        + [
            pl.BlockSpec((tile, LANES), lambda t, ids: (t, skip + ids[0])),
            pl.BlockSpec((tile, LANES), lambda t, ids: (t, skip + ids[1])),
        ]
        + [pl.BlockSpec((width, panel), whole)] * 2
        + [pl.BlockSpec((tile, width), by_tile)] * (2 * chunks)
    )
    aliases = {}
    if role != "first":
        if role == "middle":
            aliases = {len(operands) + 1: 0}
        operands.append(total)
        in_specs.append(pl.BlockSpec((tile, panel), by_tile))
    if role == "last":
        operands += [*squares, *rows_in]
        in_specs += [pl.BlockSpec((tile, LANES), by_tile)] * chunks
        in_specs += [pl.BlockSpec((1, tile), by_lane)] * 2
        out_specs = [pl.BlockSpec((1, tile), by_lane), pl.BlockSpec((8, groups), whole)]
        out_shape = [
            jax.ShapeDtypeStruct((1, rows), F32),
            jax.ShapeDtypeStruct((8, groups), F32),
        ]
    else:
        out_specs = pl.BlockSpec((tile, panel), by_tile)
        out_shape = jax.ShapeDtypeStruct((rows, panel), F32)
    return pl.pallas_call(
        functools.partial(second_kernel, chunks, role),
        grid_spec=pltpu.PrefetchScalarGridSpec(
            num_scalar_prefetch=1,
            grid=(rows // tile,),
            in_specs=in_specs,
            out_specs=out_specs,
            scratch_shapes=[pltpu.VMEM((width, panel), BF16)] * 2,
        ),
        out_shape=out_shape,
        input_output_aliases=aliases,
        cost_estimate=pl.CostEstimate(
            flops=12 * rows * panel * width, bytes_accessed=12 * rows * panel, transcendentals=0
        ),
        name="second_chunk_" + role,
    )(ids, *operands)


def slots_of(group_ids, owner_slots):
    member_of = group_ids == lax.iota(jnp.int32, owner_slots.shape[0])[None, :]
    return jnp.sum(jnp.where(member_of, owner_slots[None, :], 0), axis=1)


def ring_device(
    count, correlations, first_inverse, off_block, second_inverse, ard_mean, group_ids, owner_slots
):
    panel = first_inverse.shape[1]
    tile = min(512, correlations.shape[0])
    chips = count // 2
    slabs = chips // 2

    def chip_at(position):
        position = position % chips
        return 2 * position if position < slabs else 2 * (2 * slabs - 1 - position) + 1

    def ring(step):
        return [
            (2 * chip_at(p) + core, 2 * chip_at(p + step) + core)
            for p in range(chips)
            for core in range(2)
        ]

    def send(value, pairs):
        return lax.ppermute(value, "cand", pairs)

    partner = [(i, i ^ 1) for i in range(count)]
    index = lax.axis_index("cand")
    core, chip = index % 2, index // 2
    position = jnp.where(chip % 2 == 0, chip // 2, 2 * slabs - 1 - chip // 2)

    def block(offset):
        there = (position + offset + chips) % chips
        return jnp.where(there < slabs, 2 * there, 2 * (2 * slabs - 1 - there) + 1)

    column = lax.broadcasted_iota(jnp.int32, (1, panel + LANES), 1) // LANES
    packed = jnp.where(
        column <= chip,
        jnp.pad(first_inverse, ((0, 0), (0, LANES))),
        jnp.pad(second_inverse.T, ((0, 0), (LANES, 0))),
    )

    half = chips // 2
    ways = (ring(1), ring(-1))

    def gather(own, lone):
        held = {0: own}
        for hop in range(1, half + 1):
            for way, sign in ((0, -1), (1, 1)):
                if hop == half and way != lone:
                    continue
                came_from = held[sign * (hop - 1)]
                held[sign * hop] = send(came_from, ways[way])
        other = {key: send(value, partner) for key, value in held.items()}
        return held, other

    firsts, firsts_other = gather(packed, 0)
    offs, offs_other = gather(off_block, 1)
    chunks = [(-hop, hop) for hop in range(1, half)] + [(0, half)]

    def pick(held, other, pair):
        keys = [key if key in held else -key for key in pair]
        return [array for key in keys for array in (held[key], other[key])]

    blocks = [block(key) for pair in chunks for key in pair]
    high, low, energies = prepare(correlations, ard_mean[None, :], panel, 256)
    fs, squares, solves, ids = [], [], [], []
    for i, pair in enumerate(chunks):
        ids.append(jnp.stack([blocks[2 * i], blocks[2 * i + 1], core, *blocks]).astype(jnp.int32))
        fs_high, fs_low, square, solve_high, solve_low = first_chunk(
            ids[i], pick(firsts, firsts_other, pair), high, low, tile
        )
        fs.append((fs_high, fs_low))
        squares.append(square)
        solves.append((solve_high, solve_low))
    slots = slots_of(group_ids, owner_slots)[None, :].astype(jnp.int32)
    total = None
    for i, pair in enumerate(chunks):
        role = "first" if i == 0 else "last" if i == len(chunks) - 1 else "middle"
        pieces = pick(offs, offs_other, pair)
        extra = {}
        if role == "last":
            extra = dict(squares=squares, rows_in=(energies, slots), groups=owner_slots.shape[0])
        total = second_chunk(role, ids[i], pieces, correlations, solves[i], fs, tile, total=total, **extra)
    variances, sums = total
    step = 1
    while step < count:
        sums = sums + send(sums, [(i, i ^ step) for i in range(count)])
        step *= 2
    owned = owner_slots.shape[0] // count
    mine = lax.dynamic_slice_in_dim(sums, index * owned, owned, axis=1)
    return energies[0], variances[0], mine[0] / mine[2], mine[1] / mine[2]


def matmul_t(left, right):
    return lax.dot_general(
        left,
        right,
        (((1,), (1,)), ((), ())),
        precision=lax.Precision.HIGHEST,
        preferred_element_type=jnp.float32,
    )


def gather_device(
    correlations, first_inverse, off_block, second_inverse, ard_mean, group_ids, owner_slots
):
    panel_width = first_inverse.shape[1]
    leading = correlations[:, :panel_width]
    trailing = correlations[:, panel_width:]
    first_solve = matmul_t(leading, lax.all_gather(first_inverse, "cand", axis=0, tiled=True))
    second_full = lax.all_gather(second_inverse, "cand", axis=1, tiled=True)
    residual = trailing - matmul_t(
        first_solve, lax.all_gather(off_block, "cand", axis=0, tiled=True)
    )
    second_solve = matmul_t(residual, second_full)
    variances = jnp.sum(first_solve * first_solve, axis=1) + jnp.sum(
        second_solve * second_solve, axis=1
    )
    energies = jnp.dot(
        correlations, ard_mean, precision=lax.Precision.HIGHEST, preferred_element_type=jnp.float32
    )
    group_count = owner_slots.shape[0]
    slot_of = slots_of(group_ids, owner_slots)
    selector = (slot_of[:, None] == lax.iota(jnp.int32, group_count)[None, :]).astype(jnp.float32)
    moments = jnp.stack([energies, variances, jnp.ones_like(energies)], axis=0)
    partial_sums = jnp.dot(
        moments, selector, precision=lax.Precision.HIGHEST, preferred_element_type=jnp.float32
    )
    owned_sums = lax.psum_scatter(partial_sums, "cand", scatter_dimension=1, tiled=True)
    group_energy = owned_sums[0] / owned_sums[2]
    group_variance = owned_sums[1] / owned_sums[2]
    return (energies, variances, group_energy, group_variance)


def solution(mesh):
    placed = (
        P(("groups", "cand"), None),
        P(("groups", "cand"), None),
        P(("groups", "cand"), None),
        P("groups", "cand"),
        P("groups"),
        P(("groups", "cand"), None),
        P("groups"),
    )
    count = mesh.shape["cand"]

    def per_device(*arrays):
        panel = arrays[1].shape[1]
        fits = (
            2 * panel == LANES * count
            and count % 8 == 0
            and arrays[0].shape[0] % 512 == 0
            and arrays[6].shape[0] % LANES == 0
        )
        if fits:
            return ring_device(count, *arrays)
        return gather_device(*arrays)

    return jax.shard_map(
        per_device,
        mesh=mesh,
        in_specs=placed,
        out_specs=(
            P(("groups", "cand")),
            P(("groups", "cand")),
            P(("groups", "cand")),
            P(("groups", "cand")),
        ),
        check_vma=False,
    )
```
